256 devices in a mesh: row: 8 (over y, core), box: 32 (over z, x).
Axes of the slice: x: 4, y: 4, z: 8, core: 2. Of those that a mesh axis runs over, the one named last changes fastest.
Arguments:
- solved: bfloat16 [2, 32768, 512], P(None, ('box', 'row')), may hold values from -6 to 6
- rhs: bfloat16 [8, 32768, 512], P('row', 'box'), may hold values from -6 to 6
- leaf_basis: bfloat16 [8, 3, 128, 256, 128], P('row', None, 'box'), may hold values from -0.375 to 0.375
- first_level: bfloat16 [8, 3, 32, 4, 4, 128, 128], P('row', None, 'box'), may hold values from -0.25 to 0.25
- second_level: bfloat16 [8, 3, 32, 32, 128, 128], P('row', None, 'box'), may hold values from -0.5 to 0.5
- third_level: bfloat16 [8, 3, 32, 32, 128, 128], P('row', None, 'box'), may hold values from -0.25 to 0.25
- fourth_level: bfloat16 [8, 3, 32, 2, 8, 128, 128], P('row', None, 'box'), may hold values from -0.1875 to 0.1875
- out_basis: bfloat16 [8, 3, 64, 512, 128], P('row', None, 'box'), may hold values from -0.5 to 0.5
Outputs:
- unknowns: bfloat16 [8, 32768, 512], P('row', 'box')
The draws below stay inside these ranges and needn't reach their ends.
All inputs are finite; a program needn't handle non-finite values.
Results may differ from the reference program's by a relative error of at most 0.015.
Values may be sent and summed in bfloat16 or wider, within the bound.
A program may use at most 128 MiB of HBM per device.

```python
import jax
import jax.numpy as jnp
from jax import lax

LEAF = 256
R = 128
NRHS = 512
BLK = 32768
GROUPS = 8
N_BOX = 32


def level_of(own_key, shape, split, least, top_value):
    factor_of, own = 1.0, jax.random.fold_in(own_key, 6)
    for axis_at, blocks in split:
        heights = jnp.exp(jax.random.uniform(jax.random.fold_in(own, axis_at), (blocks,), jnp.float32, least / len(split), top_value / len(split)))
        factor_of = factor_of * jnp.repeat(heights, shape[axis_at] // blocks).reshape([-1 if axis == axis_at else 1 for axis in range(len(shape))])
    return factor_of


def centred(key, dims, spread, limit, cuts=(), held_as=jnp.bfloat16):
    array = jax.random.normal(key, dims, jnp.float32) * spread
    if len(cuts) > 0:
        array = level_of(key, dims, cuts, -0.22, 0.18) * array
    return jnp.clip(array, min=-limit, max=limit).astype(held_as)


def setup_inputs(seed: int = 0) -> dict:
    splits = jax.random.split(jax.random.key(seed), 9)
    solved = centred(splits[0], (2, BLK, NRHS), 1.0, 6.0, ((1, 256),))
    rhs = centred(splits[1], (GROUPS, BLK, NRHS), 1.0, 6.0, ((0, 8), (1, 32)))
    leaf_basis = centred(splits[2], (GROUPS, 3, 4 * N_BOX, LEAF, R), LEAF ** -0.5, 0.375, ((0, 8), (2, 32)))
    first_level = centred(splits[3], (GROUPS, 3, N_BOX, 4, 4, R, R), (4 * R) ** -0.5, 0.25, ((0, 8), (2, 32)))
    second_level = centred(splits[4], (GROUPS, 3, N_BOX, N_BOX, R, R), R ** -0.5, 0.5, ((0, 8), (2, 32)))
    third_level = centred(splits[5], (GROUPS, 3, N_BOX, N_BOX, R, R), (4 * R) ** -0.5, 0.25, ((0, 8), (2, 32)))
    fourth_level = centred(splits[6], (GROUPS, 3, N_BOX, 2, N_BOX // 4, R, R), (R * N_BOX // 4) ** -0.5, 0.1875, ((0, 8), (2, 32)))
    out_basis = centred(splits[7], (GROUPS, 3, 2 * N_BOX, 2 * LEAF, R), R ** -0.5, 0.5, ((0, 8), (2, 32)))
    return dict(solved=solved, rhs=rhs, leaf_basis=leaf_basis, first_level=first_level, second_level=second_level, third_level=third_level, fourth_level=fourth_level, out_basis=out_basis)


def as_float(value):
    return value.astype(jnp.float32)


def apply_butterfly(inputs, basis, first_mats, second_mats, third_mats, fourth_mats, outer_basis):
    columns = inputs.shape[-1]
    leaf_coef = jnp.einsum('lpr,lpn->lrn', as_float(basis), as_float(inputs.reshape(4 * N_BOX, LEAF, columns))).astype(jnp.bfloat16)
    mid_coef = jnp.einsum('dskrq,dkqn->dsrn', as_float(first_mats), as_float(leaf_coef.reshape(N_BOX, 4, R, columns))).astype(jnp.bfloat16)
    slot_coef = jnp.einsum('dstrq,dsqn->dstrn', as_float(second_mats.reshape(N_BOX, 4, N_BOX // 4, R, R)), as_float(mid_coef)).astype(jnp.bfloat16)
    slot_coef = slot_coef.reshape(N_BOX // 4, 4, N_BOX, R, columns)
    group_coef = jnp.einsum('egkrq,gkeqn->egrn', as_float(third_mats.reshape(N_BOX, N_BOX // 4, 4, R, R)), as_float(slot_coef)).astype(jnp.bfloat16)
    half_coef = jnp.einsum('ehgrq,egqn->ehrn', as_float(fourth_mats), as_float(group_coef)).astype(jnp.bfloat16)
    result = jnp.einsum('ehpr,ehrn->ehpn', as_float(outer_basis.reshape(N_BOX, 2, 2 * LEAF, R)), as_float(half_coef))
    return result.reshape(4 * LEAF * N_BOX, columns)


def reference(solved, rhs, leaf_basis, first_level, second_level, third_level, fourth_level, out_basis):
    def one_group(item):
        rhs_rows, basis, first_mats, second_mats, third_mats, fourth_mats, outer_basis = item

        def butterfly(which, inputs):
            return apply_butterfly(inputs, basis[which], first_mats[which], second_mats[which], third_mats[which], fourth_mats[which], outer_basis[which])

        residual = as_float(rhs_rows) - butterfly(0, solved[0]) - butterfly(1, solved[1])
        residual_b = residual.astype(jnp.bfloat16)
        return (residual + butterfly(2, residual_b)).astype(jnp.bfloat16)

    return lax.map(one_group, (rhs, leaf_basis, first_level, second_level, third_level, fourth_level, out_basis))
```

```python
import jax
import jax.numpy as jnp
from jax import lax
from jax.sharding import PartitionSpec as P

F32 = jnp.float32
BF16 = jnp.bfloat16
NX = 4


def dot(spec, a, b):
    return jnp.einsum(spec, a, b, preferred_element_type=F32)


def on_device(n_box, solved, rhs, leaf_basis, first_level, second_level, third_level, fourth_level, out_basis):
    nz = n_box // NX
    along_z = [[z * NX + x for z in range(nz)] for x in range(NX)]
    along_x = [[z * NX + x for x in range(NX)] for z in range(nz)]
    gathered = lax.all_gather(solved, "row", axis=1, tiled=True)
    basis, first, second = leaf_basis[0], first_level[0, :, 0], second_level[0, :, 0]
    third, fourth, outer = third_level[0, :, 0], fourth_level[0, :, 0], out_basis[0]
    rank = basis.shape[-1]
    third = third.reshape(3, nz, NX, rank, rank)
    outer_w = dot("jhqab,jqkbc->kjhaqc", fourth, third).astype(BF16)
    outer_w = lax.all_to_all(outer_w, "box", 0, 0, axis_index_groups=along_x, tiled=True)
    second = second.reshape(3, nz, NX, rank, rank)
    second = lax.all_to_all(second, "box", 1, 1, axis_index_groups=along_z, tiled=True)
    full = dot("xjhaqc,jqxcd->jxhaqd", outer_w, second).astype(BF16)
    full = full.reshape(3, NX, 2 * rank, nz * rank)

    def middle(js, inputs):
        n = inputs.shape[0]
        columns = inputs.shape[-1]
        leaf = dot("jlpr,jlpn->jlrn", basis[js], inputs.reshape(n, 4, -1, columns)).astype(BF16)
        mid = dot("jskrq,jkqn->jsrn", first[js], leaf).astype(BF16)
        mid = jnp.repeat(mid, nz // 4, axis=1)
        mid = lax.all_to_all(mid, "box", 1, 1, axis_index_groups=along_z, tiled=True)
        part = dot("jxab,jbn->jxan", full[js], mid.reshape(n, nz * rank, columns)).astype(BF16)
        part = lax.all_to_all(part, "box", 1, 1, axis_index_groups=along_x, tiled=True)
        half = part.astype(F32).sum(1).astype(BF16).reshape(n, 2, rank, columns)
        return dot("jhpr,jhrn->jhpn", outer[js], half).reshape(n, -1, columns)

    both = middle(slice(0, 2), gathered)
    residual = rhs[0].astype(F32) - both[0] - both[1]
    correction = middle(slice(2, 3), residual.astype(BF16)[None])[0]
    return (residual + correction).astype(BF16)[None]


def solution(mesh):
    placed = (
        P(None, ("box", "row"), None),
        P("row", "box", None),
        P("row", None, "box", None, None),
        P("row", None, "box", None, None, None, None),
        P("row", None, "box", None, None, None),
        P("row", None, "box", None, None, None),
        P("row", None, "box", None, None, None, None),
        P("row", None, "box", None, None),
    )

    def run(*args):
        return on_device(mesh.shape["box"], *args)

    return jax.shard_map(run, mesh=mesh, in_specs=placed, out_specs=P("row", "box", None), check_vma=False)
```

```python
import functools

import jax
import jax.numpy as jnp
from jax import lax
from jax.experimental import pallas as pl
from jax.experimental.pallas import tpu as pltpu
from jax.sharding import PartitionSpec as P

F32 = jnp.float32
BF16 = jnp.bfloat16
MESH = pl.DeviceIdType.MESH
NX, NZ, NY = 4, 8, 4
X_DISTS = (2, 1, 3)
Z_DISTS = (4, 3, 5, 2, 6, 1, 7)
RANK, COLS = 128, 512


def dot(a, b):
    return jnp.dot(a, b, preferred_element_type=F32)


def kernel(
    solved, rhs, leaf, first, second, third, fourth, outer, out,
    gath, leaf_v, leaf_t, first_v, third_v, fourth_v, outer_v, rhs_v,
    w_send, w_recv, sec, full, leaf_c, m_send, m_recv, p_send, p_recv, half, res, res_b,
    load_sem, own_sem, ag_s, ag_r, w_s, w_r, sec_s, sec_r, m_s, m_r, p_s, p_r,
):
    row, box = lax.axis_index("row"), lax.axis_index("box")
    y, core = row // 2, row % 2
    z, x = box // NX, box % NX

    def at_z(plane):
        return (row, plane * NX + x)

    def at_x(col):
        return (row, z * NX + col)

    def at_y(chip):
        return (chip * 2 + core, box)

    partner = (y * 2 + 1 - core, box)
    other_z = z + 1 - 2 * (z % 2)

    def remote(src, dst, send, recv, device):
        return pltpu.make_async_remote_copy(
            src_ref=src, dst_ref=dst, send_sem=send, recv_sem=recv, device_id=device, device_id_type=MESH
        )

    barrier = pltpu.get_barrier_semaphore()
    peers = [partner] + [at_y((y + i) % NY) for i in range(1, NY)]
    peers += [at_x((x + i) % NX) for i in range(1, NX)] + [at_z((z + i) % NZ) for i in range(1, NZ)]
    for peer in peers:
        pl.semaphore_signal(barrier, inc=1, device_id=peer, device_id_type=MESH)

    loads = [
        (third.at[0, 0, 0], third_v.at[0]),
        (fourth.at[0, 0, 0], fourth_v.at[0]),
        (third.at[0, 1, 0], third_v.at[1]),
        (fourth.at[0, 1, 0], fourth_v.at[1]),
        (third.at[0, 2, 0], third_v.at[2]),
        (fourth.at[0, 2, 0], fourth_v.at[2]),
        (leaf.at[0], leaf_v),
        (first.at[0, :, 0], first_v),
        (solved, gath.at[:, row]),
        (outer.at[0], outer_v),
        (rhs.at[0], rhs_v),
        (second.at[0, 0, 0, pl.ds(z * NX, NX)], sec.at[0, z]),
        (second.at[0, 1, 0, pl.ds(z * NX, NX)], sec.at[1, z]),
        (second.at[0, 2, 0, pl.ds(z * NX, NX)], sec.at[2, z]),
    ]
    loads = [pltpu.make_async_copy(src, dst, load_sem.at[i]) for i, (src, dst) in enumerate(loads)]
    for copy in loads:
        copy.start()
    pl.semaphore_wait(barrier, len(peers))

    sends = []

    def start(copy):
        copy.start()
        sends.append(copy)

    for n, i in enumerate((1, 3, 2)):
        start(remote(solved, gath.at[:, row], ag_s.at[n], ag_r.at[row], at_y((y + i) % NY)))
    start(remote(solved, gath.at[:, row], ag_s.at[3], ag_r.at[row], partner))

    def send_second(j):
        for n, i in enumerate(Z_DISTS):
            plane = (z + i) % NZ
            start(remote(second.at[0, j, 0, pl.ds(plane * NX, NX)], sec.at[j, z], sec_s.at[j, n], sec_r.at[j, n], at_z(plane)))

    def wait_second(j):
        for n, i in enumerate(Z_DISTS):
            plane = (z - i + NZ) % NZ
            remote(sec.at[j, plane], sec.at[j, plane], sec_s.at[j, n], sec_r.at[j, n], at_z(plane)).wait_recv()
        loads[11 + j].wait()

    def outer_weights(j):
        loads[2 * j].wait()
        loads[2 * j + 1].wait()

        @pl.loop(0, NZ)
        def _(q):
            a = fourth_v[j, :, q].reshape(2 * RANK, RANK)
            b = jnp.concatenate([third_v[j, q * NX + k] for k in range(NX)], axis=1)
            o = dot(a, b).astype(BF16)
            for k in range(NX):
                w_send[j, k, q] = o[:, k * RANK : (k + 1) * RANK]

        for n, i in enumerate(X_DISTS):
            col = (x + i) % NX
            start(remote(w_send.at[j, col], w_recv.at[j, x], w_s.at[j, n], w_r.at[j, n], at_x(col)))
        pltpu.make_async_copy(w_send.at[j, x], w_recv.at[j, x], own_sem.at[j]).start()

    def wait_weights(j):
        for n, i in enumerate(X_DISTS):
            col = (x - i + NX) % NX
            remote(w_recv.at[j, col], w_recv.at[j, col], w_s.at[j, n], w_r.at[j, n], at_x(col)).wait_recv()
        pltpu.make_async_copy(w_send.at[j, x], w_recv.at[j, x], own_sem.at[j]).wait()

    def full_weights(j):
        wait_second(j)
        wait_weights(j)

        @pl.loop(0, NX)
        def _(c):
            for q in range(NZ):
                full[j, pl.ds(c * 2 * RANK, 2 * RANK), q * RANK : (q + 1) * RANK] = dot(
                    w_recv[j, c, q], sec[j, q, c]
                ).astype(BF16)

    def leaf_levels(j, rows_of):
        for l in range(4):
            leaf_c[j, l * RANK : (l + 1) * RANK] = dot(leaf_t[j, l], rows_of(l)).astype(BF16)
        a = jnp.concatenate([first_v[j, :, k].reshape(4 * RANK, RANK) for k in range(4)], axis=1)
        m_send[j] = dot(a, leaf_c[j]).astype(BF16).reshape(4, RANK, COLS)

    pair, odd = z // 2, z % 2
    near = [(z + 2 - odd) % NZ, (z + 5 - 2 * odd) % NZ, (z + 7 - odd) % NZ]
    side = 2 * odd - 1

    def send_mid(j):
        for t, plane in enumerate(near):
            s = (pair + t + 1) % 4
            start(remote(m_send.at[j, s], m_recv.at[j, z], m_s.at[j, t], m_r.at[j, z], at_z(plane)))
        start(remote(m_send.at[j, pair], m_recv.at[j, z], m_s.at[j, 3], m_r.at[j, z], at_z(other_z)))
        pltpu.make_async_copy(m_send.at[j, pair], m_recv.at[j, z], own_sem.at[3 + j]).start()

    def pass_mid(j):
        for n, i in enumerate((1, 2, 3)):
            plane = (z + side * i + NZ) % NZ
            here = m_recv.at[j, plane]
            remote(here, here, m_s.at[j, 4 + n], m_r.at[j, plane], at_z(plane)).wait_recv()
            start(remote(here, here, m_s.at[j, 4 + n], m_r.at[j, plane], at_z(other_z)))

    def wait_mid(j):
        for i in (1, 2, 3, 4):
            plane = (z - side * i + NZ) % NZ
            here = m_recv.at[j, plane]
            remote(here, here, m_s.at[j, 4], m_r.at[j, plane], at_z(plane)).wait_recv()
        pltpu.make_async_copy(m_send.at[j, pair], m_recv.at[j, z], own_sem.at[3 + j]).wait()

    def partial(j):
        for n, i in enumerate(X_DISTS + (0,)):
            col = (x + i) % NX
            a = full[j, pl.ds(pl.multiple_of(col * 2 * RANK, 2 * RANK), 2 * RANK)]
            p_send[j, col] = dot(a, m_recv[j].reshape(NZ * RANK, COLS)).astype(BF16)
            if i:
                start(remote(p_send.at[j, col], p_recv.at[j, n], p_s.at[j, n], p_r.at[j, n], at_x(col)))

    def halves(j):
        total = p_send[j, x].astype(F32)
        for n in range(3):
            here = p_recv.at[j, n]
            remote(here, here, p_s.at[j, n], p_r.at[j, n], at_x(x)).wait_recv()
            total += p_recv[j, n].astype(F32)
        half[j] = total.astype(BF16)

    send_second(0)
    send_second(1)
    outer_weights(0)
    outer_weights(1)
    outer_weights(2)
    loads[6].wait()
    for j in range(3):
        for l in range(4):
            leaf_t[j, l] = leaf_v[j, l].T
    loads[7].wait()
    loads[8].wait()
    for n, i in enumerate((1, 3, 2)):
        chip = ((y - i + NY) % NY) * 2 + core
        here = gath.at[:, chip]
        remote(here, here, ag_s.at[4 + n], ag_r.at[chip], partner).wait_recv()
        start(remote(here, here, ag_s.at[4 + n], ag_r.at[chip], partner))
    for i in (0, 1, 3, 2):
        chip = ((y - i + NY) % NY) * 2 + 1 - core
        here = gath.at[:, chip]
        remote(here, here, ag_s.at[0], ag_r.at[chip], partner).wait_recv()
    for j in range(2):
        leaf_levels(j, lambda l: gath[j, 2 * l : 2 * l + 2].reshape(2 * RANK, COLS))
        send_mid(j)
    full_weights(0)
    pass_mid(0)
    full_weights(1)
    wait_mid(0)
    partial(0)
    pass_mid(1)
    send_second(2)
    wait_mid(1)
    partial(1)
    halves(0)
    loads[9].wait()
    loads[10].wait()
    halves(1)
    for h in range(2):
        here = pl.ds(h * 4 * RANK, 4 * RANK)
        a = jnp.concatenate([outer_v[0, h], outer_v[1, h]], axis=1)
        b = jnp.concatenate([half[0, h * RANK : (h + 1) * RANK], half[1, h * RANK : (h + 1) * RANK]], axis=0)
        value = rhs_v[here].astype(F32) - dot(a, b)
        res[here] = value
        res_b[here] = value.astype(BF16)
    leaf_levels(2, lambda l: res_b[l * 2 * RANK : (l + 1) * 2 * RANK])
    send_mid(2)
    full_weights(2)
    pass_mid(2)
    wait_mid(2)
    partial(2)
    halves(2)
    for h in range(2):
        here = pl.ds(h * 4 * RANK, 4 * RANK)
        out[0, here] = (res[here] + dot(outer_v[2, h], half[2, h * RANK : (h + 1) * RANK])).astype(BF16)
    for copy in sends:
        copy.wait_send()


def on_device(*args):
    vmem = pltpu.VMEM
    dma = pltpu.SemaphoreType.DMA
    return pl.pallas_call(
        kernel,
        out_shape=jax.ShapeDtypeStruct((1, 1024, COLS), BF16),
        in_specs=[pl.BlockSpec(memory_space=pl.ANY)] * 8,
        out_specs=pl.BlockSpec(memory_space=pltpu.VMEM),
        scratch_shapes=[
            vmem((2, 8, RANK, COLS), BF16),
            vmem((3, 4, 2 * RANK, RANK), BF16),
            vmem((3, 4, RANK, 2 * RANK), BF16),
            vmem((3, 4, 4, RANK, RANK), BF16),
            vmem((3, 32, RANK, RANK), BF16),
            vmem((3, 2, NZ, RANK, RANK), BF16),
            vmem((3, 2, 4 * RANK, RANK), BF16),
            vmem((1024, COLS), BF16),
            vmem((3, NX, NZ, 2 * RANK, RANK), BF16),
            vmem((3, NX, NZ, 2 * RANK, RANK), BF16),
            vmem((3, NZ, NX, RANK, RANK), BF16),
            vmem((3, 8 * RANK, 8 * RANK), BF16),
            vmem((3, 4 * RANK, COLS), BF16),
            vmem((3, 4, RANK, COLS), BF16),
            vmem((3, NZ, RANK, COLS), BF16),
            vmem((3, NX, 2 * RANK, COLS), BF16),
            vmem((3, 3, 2 * RANK, COLS), BF16),
            vmem((3, 2 * RANK, COLS), BF16),
            vmem((1024, COLS), F32),
            vmem((1024, COLS), BF16),
            dma((14,)),
            dma((6,)),
            dma((7,)),
            dma((8,)),
            dma((3, 3)),
            dma((3, 3)),
            dma((3, 7)),
            dma((3, 7)),
            dma((3, 7)),
            dma((3, 8)),
            dma((3, 3)),
            dma((3, 3)),
        ],
        compiler_params=pltpu.CompilerParams(
            collective_id=0, has_side_effects=True, vmem_limit_bytes=67043328
        ),
    )(*args)


def solution(mesh):
    placed = (
        P(None, ("box", "row"), None),
        P("row", "box", None),
        P("row", None, "box", None, None),
        P("row", None, "box", None, None, None, None),
        P("row", None, "box", None, None, None),
        P("row", None, "box", None, None, None),
        P("row", None, "box", None, None, None, None),
        P("row", None, "box", None, None),
    )
    return jax.shard_map(on_device, mesh=mesh, in_specs=placed, out_specs=P("row", "box", None), check_vma=False)
```

```python
import functools

import jax
import jax.numpy as jnp
from jax import lax
from jax.experimental import pallas as pl
from jax.experimental.pallas import tpu as pltpu
from jax.sharding import PartitionSpec as P

F32 = jnp.float32
BF16 = jnp.bfloat16
MESH = pl.DeviceIdType.MESH
NX, NZ, NY = 4, 8, 4
X_DISTS = (2, 1, 3)
Z_DISTS = (4, 3, 5, 2, 6, 1, 7)
RANK, COLS = 128, 512
EARLY, LATE = 2, 4


def dot(a, b):
    return jnp.dot(a, b, preferred_element_type=F32)


def kernel(
    solved, rhs, leaf, first, second, third, fourth, outer, out,
    gath, leaf_v, leaf_t, first_v, third_v, fourth_v, outer_v, rhs_v,
    w_send, w_recv, sec, full, half, res, res_b, out_v,
    m_send0, m_recv0, p_send0, p_recv0, m_send1, m_recv1, p_send1, p_recv1,
    load_sem, own_sem, out_sem, ag_s, ag_r, w_s, w_r, sec_s, sec_r,
    m_s0, m_r0, p_s0, p_r0, own0, m_s1, m_r1, p_s1, p_r1, own1,
):
    early = (m_send0, m_recv0, p_send0, p_recv0, m_s0, m_r0, p_s0, p_r0, own0, EARLY, 0)
    late = (m_send1, m_recv1, p_send1, p_recv1, m_s1, m_r1, p_s1, p_r1, own1, LATE, 2)

    def unit(j, c):
        *refs, chunks, base = late if j == 2 else early
        return (*refs, (j - base) * chunks + c)

    def cut(j, c):
        width = COLS // (LATE if j == 2 else EARLY)
        return slice(c * width, (c + 1) * width)

    row, box = lax.axis_index("row"), lax.axis_index("box")
    y, core = row // 2, row % 2
    z, x = box // NX, box % NX

    def at_z(plane):
        return (row, plane * NX + x)

    def at_x(col):
        return (row, z * NX + col)

    def at_y(chip):
        return (chip * 2 + core, box)

    partner = (y * 2 + 1 - core, box)
    other_z = z + 1 - 2 * (z % 2)

    def remote(src, dst, send, recv, device):
        return pltpu.make_async_remote_copy(
            src_ref=src, dst_ref=dst, send_sem=send, recv_sem=recv, device_id=device, device_id_type=MESH
        )

    barrier = pltpu.get_barrier_semaphore()
    peers = [partner] + [at_y((y + i) % NY) for i in range(1, NY)]
    peers += [at_x((x + i) % NX) for i in range(1, NX)] + [at_z((z + i) % NZ) for i in range(1, NZ)]
    for peer in peers:
        pl.semaphore_signal(barrier, inc=1, device_id=peer, device_id_type=MESH)

    loads = [
        (third.at[0, 0, 0], third_v.at[0]),
        (fourth.at[0, 0, 0], fourth_v.at[0]),
        (third.at[0, 1, 0], third_v.at[1]),
        (fourth.at[0, 1, 0], fourth_v.at[1]),
        (third.at[0, 2, 0], third_v.at[2]),
        (fourth.at[0, 2, 0], fourth_v.at[2]),
        (leaf.at[0], leaf_v),
        (first.at[0, :, 0], first_v),
        (solved, gath.at[:, row]),
        (outer.at[0], outer_v),
        (rhs.at[0], rhs_v),
        (second.at[0, 0, 0, pl.ds(z * NX, NX)], sec.at[0, z]),
        (second.at[0, 1, 0, pl.ds(z * NX, NX)], sec.at[1, z]),
        (second.at[0, 2, 0, pl.ds(z * NX, NX)], sec.at[2, z]),
    ]
    loads = [pltpu.make_async_copy(src, dst, load_sem.at[i]) for i, (src, dst) in enumerate(loads)]
    for copy in loads:
        copy.start()
    pl.semaphore_wait(barrier, len(peers))

    sends = []

    def start(copy):
        copy.start()
        sends.append(copy)

    for n, i in enumerate((1, 3, 2)):
        start(remote(solved, gath.at[:, row], ag_s.at[n], ag_r.at[row], at_y((y + i) % NY)))
    start(remote(solved, gath.at[:, row], ag_s.at[3], ag_r.at[row], partner))

    def send_second(j, begin=0, end=7):
        for n, i in list(enumerate(Z_DISTS))[begin:end]:
            plane = (z + i) % NZ
            start(remote(second.at[0, j, 0, pl.ds(plane * NX, NX)], sec.at[j, z], sec_s.at[j, n], sec_r.at[j, n], at_z(plane)))

    def wait_second(j):
        for n, i in enumerate(Z_DISTS):
            plane = (z - i + NZ) % NZ
            remote(sec.at[j, plane], sec.at[j, plane], sec_s.at[j, n], sec_r.at[j, n], at_z(plane)).wait_recv()
        loads[11 + j].wait()

    def outer_weights(j):
        loads[2 * j].wait()
        loads[2 * j + 1].wait()

        @pl.loop(0, NZ)
        def _(q):
            a = fourth_v[j, :, q].reshape(2 * RANK, RANK)
            b = jnp.concatenate([third_v[j, q * NX + k] for k in range(NX)], axis=1)
            o = dot(a, b).astype(BF16)
            for k in range(NX):
                w_send[j, k, q] = o[:, k * RANK : (k + 1) * RANK]

        for n, i in enumerate(X_DISTS):
            col = (x + i) % NX
            start(remote(w_send.at[j, col], w_recv.at[j, x], w_s.at[j, n], w_r.at[j, n], at_x(col)))
        pltpu.make_async_copy(w_send.at[j, x], w_recv.at[j, x], own_sem.at[j]).start()

    def wait_weights(j):
        for n, i in enumerate(X_DISTS):
            col = (x - i + NX) % NX
            remote(w_recv.at[j, col], w_recv.at[j, col], w_s.at[j, n], w_r.at[j, n], at_x(col)).wait_recv()
        pltpu.make_async_copy(w_send.at[j, x], w_recv.at[j, x], own_sem.at[j]).wait()

    def full_weights(j):
        wait_second(j)
        wait_weights(j)

        @pl.loop(0, NX)
        def _(c):
            for q in range(NZ):
                full[j, pl.ds(c * 2 * RANK, 2 * RANK), q * RANK : (q + 1) * RANK] = dot(
                    w_recv[j, c, q], sec[j, q, c]
                ).astype(BF16)

    def leaf_levels(j, c, rows_of):
        m_send, *_, u = unit(j, c)
        coef = jnp.concatenate([dot(leaf_t[j, l], rows_of(l)).astype(BF16) for l in range(4)], axis=0)
        a = jnp.concatenate([first_v[j, :, k].reshape(4 * RANK, RANK) for k in range(4)], axis=1)
        m_send[u] = dot(a, coef).astype(BF16).reshape(4, RANK, -1)

    pair, odd = z // 2, z % 2
    near = [(z + 2 - odd) % NZ, (z + 5 - 2 * odd) % NZ, (z + 7 - odd) % NZ]
    side = 2 * odd - 1

    def own_mid(j, c):
        m_send, m_recv, _, _, _, _, _, _, own, u = unit(j, c)
        return pltpu.make_async_copy(m_send.at[u, pair], m_recv.at[u, z], own.at[u])

    def send_mid(j, c):
        m_send, m_recv, _, _, m_s, m_r, _, _, _, u = unit(j, c)
        for t, plane in enumerate(near):
            s = (pair + t + 1) % 4
            start(remote(m_send.at[u, s], m_recv.at[u, z], m_s.at[u, t], m_r.at[u, z], at_z(plane)))
        start(remote(m_send.at[u, pair], m_recv.at[u, z], m_s.at[u, 3], m_r.at[u, z], at_z(other_z)))
        own_mid(j, c).start()

    def pass_mid(j, c):
        _, m_recv, _, _, m_s, m_r, _, _, _, u = unit(j, c)
        for n, i in enumerate((1, 2, 3)):
            plane = (z + side * i + NZ) % NZ
            here = m_recv.at[u, plane]
            remote(here, here, m_s.at[u, 4 + n], m_r.at[u, plane], at_z(plane)).wait_recv()
            start(remote(here, here, m_s.at[u, 4 + n], m_r.at[u, plane], at_z(other_z)))

    def wait_mid(j, c):
        _, m_recv, _, _, m_s, m_r, _, _, _, u = unit(j, c)
        for i in (1, 2, 3, 4):
            plane = (z - side * i + NZ) % NZ
            here = m_recv.at[u, plane]
            remote(here, here, m_s.at[u, 4], m_r.at[u, plane], at_z(plane)).wait_recv()
        own_mid(j, c).wait()

    def partial(j, c):
        _, m_recv, p_send, p_recv, _, _, p_s, p_r, _, u = unit(j, c)
        for n, i in enumerate(X_DISTS + (0,)):
            col = (x + i) % NX
            a = full[j, pl.ds(pl.multiple_of(col * 2 * RANK, 2 * RANK), 2 * RANK)]
            p_send[u, col] = dot(a, m_recv[u].reshape(NZ * RANK, -1)).astype(BF16)
            if i:
                start(remote(p_send.at[u, col], p_recv.at[u, n], p_s.at[u, n], p_r.at[u, n], at_x(col)))

    def halves(j, c):
        _, _, p_send, p_recv, _, _, p_s, p_r, _, u = unit(j, c)
        total = p_send[u, x].astype(F32)
        for n in range(3):
            here = p_recv.at[u, n]
            remote(here, here, p_s.at[u, n], p_r.at[u, n], at_x(x)).wait_recv()
            total += p_recv[u, n].astype(F32)
        half[j, :, cut(j, c)] = total.astype(BF16)

    def residual(c):
        for h in range(2):
            here = pl.ds(h * 4 * RANK, 4 * RANK)
            part = slice(h * RANK, (h + 1) * RANK)
            a = jnp.concatenate([outer_v[0, h], outer_v[1, h]], axis=1)
            b = jnp.concatenate([half[0, part, cut(0, c)], half[1, part, cut(1, c)]], axis=0)
            value = rhs_v[here, cut(0, c)].astype(F32) - dot(a, b)
            res[here, cut(0, c)] = value
            res_b[here, cut(0, c)] = value.astype(BF16)

    def put(c):
        return pltpu.make_async_copy(out_v.at[:, cut(2, c)], out.at[0, :, cut(2, c)], out_sem.at[c])

    def finish(c):
        for h in range(2):
            here = pl.ds(h * 4 * RANK, 4 * RANK)
            value = res[here, cut(2, c)] + dot(outer_v[2, h], half[2, h * RANK : (h + 1) * RANK, cut(2, c)])
            out_v[here, cut(2, c)] = value.astype(BF16)
        put(c).start()

    send_second(0)
    outer_weights(0)
    outer_weights(1)
    outer_weights(2)
    loads[6].wait()
    for j in range(3):
        for l in range(4):
            leaf_t[j, l] = leaf_v[j, l].T
    loads[7].wait()
    loads[8].wait()
    for n, i in enumerate((1, 3, 2)):
        chip = ((y - i + NY) % NY) * 2 + core
        here = gath.at[:, chip]
        remote(here, here, ag_s.at[4 + n], ag_r.at[chip], partner).wait_recv()
        start(remote(here, here, ag_s.at[4 + n], ag_r.at[chip], partner))
    for i in (0, 1, 3, 2):
        chip = ((y - i + NY) % NY) * 2 + 1 - core
        here = gath.at[:, chip]
        remote(here, here, ag_s.at[0], ag_r.at[chip], partner).wait_recv()
    for j in range(2):
        for c in range(EARLY):
            leaf_levels(j, c, lambda l: gath[j, 2 * l : 2 * l + 2, :, cut(j, c)].reshape(2 * RANK, -1))
            send_mid(j, c)
    send_second(1, 0, 1)
    full_weights(0)
    units = [(j, c) for j in range(2) for c in range(EARLY)]
    for n, (j, c) in enumerate(units):
        pass_mid(j, c)
        send_second(1, 1 + 6 * n // len(units), 1 + 6 * (n + 1) // len(units))
    send_second(2)
    for c in range(EARLY):
        wait_mid(0, c)
        partial(0, c)
    full_weights(1)
    for c in range(EARLY):
        wait_mid(1, c)
        partial(1, c)
    loads[9].wait()
    loads[10].wait()

    def start_late(c):
        leaf_levels(2, c, lambda l: res_b[l * 2 * RANK : (l + 1) * 2 * RANK, cut(2, c)])
        send_mid(2, c)

    for c in range(EARLY):
        halves(0, c)
        halves(1, c)
        residual(c)
        if c == 0:
            start_late(0)
            start_late(1)
    full_weights(2)
    for c in range(LATE):
        pass_mid(2, c)
        if c + 2 < LATE:
            start_late(c + 2)
        if c:
            wait_mid(2, c - 1)
            partial(2, c - 1)
        if c > 1:
            halves(2, c - 2)
            finish(c - 2)
    wait_mid(2, LATE - 1)
    partial(2, LATE - 1)
    for c in range(LATE - 2, LATE):
        halves(2, c)
        finish(c)
    for c in range(LATE):
        put(c).wait()
    for copy in sends:
        copy.wait_send()


def on_device(*args):
    vmem = pltpu.VMEM
    dma = pltpu.SemaphoreType.DMA
    groups = ((2 * EARLY, EARLY), (LATE, LATE))
    return pl.pallas_call(
        kernel,
        out_shape=jax.ShapeDtypeStruct((1, 1024, COLS), BF16),
        in_specs=[pl.BlockSpec(memory_space=pl.ANY)] * 8,
        out_specs=pl.BlockSpec(memory_space=pl.ANY),
        scratch_shapes=[
            vmem((2, 8, RANK, COLS), BF16),
            vmem((3, 4, 2 * RANK, RANK), BF16),
            vmem((3, 4, RANK, 2 * RANK), BF16),
            vmem((3, 4, 4, RANK, RANK), BF16),
            vmem((3, 32, RANK, RANK), BF16),
            vmem((3, 2, NZ, RANK, RANK), BF16),
            vmem((3, 2, 4 * RANK, RANK), BF16),
            vmem((1024, COLS), BF16),
            vmem((3, NX, NZ, 2 * RANK, RANK), BF16),
            vmem((3, NX, NZ, 2 * RANK, RANK), BF16),
            vmem((3, NZ, NX, RANK, RANK), BF16),
            vmem((3, 8 * RANK, 8 * RANK), BF16),
            vmem((3, 2 * RANK, COLS), BF16),
            vmem((1024, COLS), F32),
            vmem((1024, COLS), BF16),
            vmem((1024, COLS), BF16),
            *[ref for units, chunks in groups for ref in (
                vmem((units, 4, RANK, COLS // chunks), BF16),
                vmem((units, NZ, RANK, COLS // chunks), BF16),
                vmem((units, NX, 2 * RANK, COLS // chunks), BF16),
                vmem((units, 3, 2 * RANK, COLS // chunks), BF16),
            )],
            dma((14,)),
            dma((3,)),
            dma((LATE,)),
            dma((7,)),
            dma((8,)),
            dma((3, 3)),
            dma((3, 3)),
            dma((3, 7)),
            dma((3, 7)),
            *[ref for units, _ in groups for ref in (
                dma((units, 7)),
                dma((units, 8)),
                dma((units, 3)),
                dma((units, 3)),
                dma((units,)),
            )],
        ],
        compiler_params=pltpu.CompilerParams(
            collective_id=0, has_side_effects=True, vmem_limit_bytes=67043328
        ),
    )(*args)


def solution(mesh):
    placed = (
        P(None, ("box", "row"), None),
        P("row", "box", None),
        P("row", None, "box", None, None),
        P("row", None, "box", None, None, None, None),
        P("row", None, "box", None, None, None),
        P("row", None, "box", None, None, None),
        P("row", None, "box", None, None, None, None),
        P("row", None, "box", None, None),
    )
    return jax.shard_map(on_device, mesh=mesh, in_specs=placed, out_specs=P("row", "box", None), check_vma=False)
```

```python
import functools

import jax
import jax.numpy as jnp
from jax import lax
from jax.experimental import pallas as pl
from jax.experimental.pallas import tpu as pltpu
from jax.sharding import PartitionSpec as P

F32 = jnp.float32
BF16 = jnp.bfloat16
MESH = pl.DeviceIdType.MESH
NX, NZ, NY = 4, 8, 4
X_DISTS = (2, 1, 3)
Z_DISTS = (4, 3, 5, 2, 6, 1, 7)
RANK, COLS = 128, 512
EARLY, LATE = 2, 4


def dot(a, b):
    return jnp.dot(a, b, preferred_element_type=F32)


def kernel(
    solved, rhs, leaf, first, second, third, fourth, outer, out,
    gath, leaf_v, leaf_t, first_v, third_v, fourth_v, outer_v, rhs_v,
    w_send, w_recv, sec, full, half, res, res_b,
    m_send0, m_recv0, p_send0, p_recv0, m_send1, m_recv1, p_send1, p_recv1,
    load_sem, own_sem, ag_s, ag_r, w_s, w_r, sec_s, sec_r,
    m_s0, m_r0, p_s0, p_r0, own0, m_s1, m_r1, p_s1, p_r1, own1,
):
    early = (m_send0, m_recv0, p_send0, p_recv0, m_s0, m_r0, p_s0, p_r0, own0, EARLY, 0)
    late = (m_send1, m_recv1, p_send1, p_recv1, m_s1, m_r1, p_s1, p_r1, own1, LATE, 2)

    def unit(j, c):
        *refs, chunks, base = late if j == 2 else early
        return (*refs, (j - base) * chunks + c)

    def cut(j, c):
        width = COLS // (LATE if j == 2 else EARLY)
        return slice(c * width, (c + 1) * width)

    row, box = lax.axis_index("row"), lax.axis_index("box")
    y, core = row // 2, row % 2
    z, x = box // NX, box % NX

    def at_z(plane):
        return (row, plane * NX + x)

    def at_x(col):
        return (row, z * NX + col)

    def at_y(chip):
        return (chip * 2 + core, box)

    partner = (y * 2 + 1 - core, box)
    other_z = z + 1 - 2 * (z % 2)

    def remote(src, dst, send, recv, device):
        return pltpu.make_async_remote_copy(
            src_ref=src, dst_ref=dst, send_sem=send, recv_sem=recv, device_id=device, device_id_type=MESH
        )

    barrier = pltpu.get_barrier_semaphore()
    peers = [partner] + [at_y((y + i) % NY) for i in range(1, NY)]
    peers += [at_x((x + i) % NX) for i in range(1, NX)] + [at_z((z + i) % NZ) for i in range(1, NZ)]
    for peer in peers:
        pl.semaphore_signal(barrier, inc=1, device_id=peer, device_id_type=MESH)

    loads = [
        (third.at[0, 0, 0], third_v.at[0]),
        (fourth.at[0, 0, 0], fourth_v.at[0]),
        (third.at[0, 1, 0], third_v.at[1]),
        (fourth.at[0, 1, 0], fourth_v.at[1]),
        (third.at[0, 2, 0], third_v.at[2]),
        (fourth.at[0, 2, 0], fourth_v.at[2]),
        (leaf.at[0], leaf_v),
        (first.at[0, :, 0], first_v),
        (solved, gath.at[:, row]),
        (outer.at[0], outer_v),
        (rhs.at[0], rhs_v),
        (second.at[0, :, 0, pl.ds(z * NX, NX)], sec.at[:, z]),
    ]
    loads = [pltpu.make_async_copy(src, dst, load_sem.at[i]) for i, (src, dst) in enumerate(loads)]
    for copy in loads:
        copy.start()
    pl.semaphore_wait(barrier, len(peers))

    for n, i in enumerate((1, 3, 2)):
        remote(solved, gath.at[:, row], ag_s, ag_r.at[n], at_y((y + i) % NY)).start()
    remote(solved, gath.at[:, row], ag_s, ag_r.at[3], partner).start()

    def send_second(j, begin=0, end=7):
        for i in Z_DISTS[begin:end]:
            plane = (z + i) % NZ
            remote(second.at[0, j, 0, pl.ds(plane * NX, NX)], sec.at[j, z], sec_s, sec_r.at[j], at_z(plane)).start()

    def wait_second(j):
        remote(sec.at[j, :7], sec.at[j, :7], sec_s, sec_r.at[j], partner).wait_recv()
        if j == 0:
            loads[11].wait()

    def outer_weights(j):
        loads[2 * j].wait()
        loads[2 * j + 1].wait()

        @pl.loop(0, NZ)
        def _(q):
            a = fourth_v[j, :, q].reshape(2 * RANK, RANK)
            b = jnp.concatenate([third_v[j, q * NX + k] for k in range(NX)], axis=1)
            o = dot(a, b).astype(BF16)
            for k in range(NX):
                w_send[j, k, q] = o[:, k * RANK : (k + 1) * RANK]

        for i in X_DISTS:
            col = (x + i) % NX
            remote(w_send.at[j, col], w_recv.at[j, x], w_s, w_r.at[j], at_x(col)).start()
        pltpu.make_async_copy(w_send.at[j, x], w_recv.at[j, x], own_sem.at[j]).start()

    def wait_weights(j):
        remote(w_recv.at[j, :3], w_recv.at[j, :3], w_s, w_r.at[j], partner).wait_recv()
        pltpu.make_async_copy(w_send.at[j, x], w_recv.at[j, x], own_sem.at[j]).wait()

    def full_weights(j):
        wait_second(j)
        wait_weights(j)

        @pl.loop(0, NX)
        def _(c):
            for q in range(NZ):
                full[j, pl.ds(c * 2 * RANK, 2 * RANK), q * RANK : (q + 1) * RANK] = dot(
                    w_recv[j, c, q], sec[j, q, c]
                ).astype(BF16)

    def leaf_levels(j, c, rows_of):
        m_send, *_, u = unit(j, c)
        coef = jnp.concatenate([dot(leaf_t[j, l], rows_of(l)).astype(BF16) for l in range(4)], axis=0)
        a = jnp.concatenate([first_v[j, :, k].reshape(4 * RANK, RANK) for k in range(4)], axis=1)
        m_send[u] = dot(a, coef).astype(BF16).reshape(4, RANK, -1)

    pair, odd = z // 2, z % 2
    near = [(z + 2 - odd) % NZ, (z + 5 - 2 * odd) % NZ, (z + 7 - odd) % NZ]
    side = 2 * odd - 1

    def own_mid(j, c):
        m_send, m_recv, _, _, _, _, _, _, own, u = unit(j, c)
        return pltpu.make_async_copy(m_send.at[u, pair], m_recv.at[u, z], own.at[u])

    def send_mid(j, c):
        m_send, m_recv, _, _, m_s, m_r, _, _, _, u = unit(j, c)
        for t, (plane, n) in enumerate(zip(near, (1 - odd, 2, odd))):
            s = (pair + t + 1) % 4
            remote(m_send.at[u, s], m_recv.at[u, z], m_s, m_r.at[u, n], at_z(plane)).start()
        remote(m_send.at[u, pair], m_recv.at[u, z], m_s, m_r.at[u, 3], at_z(other_z)).start()
        own_mid(j, c).start()

    def pass_mid(j, c):
        _, m_recv, _, _, m_s, m_r, _, _, _, u = unit(j, c)
        for n, i in enumerate((1, 2, 3)):
            here = m_recv.at[u, (z + side * i + NZ) % NZ]
            remote(here, here, m_s, m_r.at[u, n], partner).wait_recv()
            remote(here, here, m_s, m_r.at[u, 3], at_z(other_z)).start()

    def wait_mid(j, c):
        _, m_recv, _, _, m_s, m_r, _, _, _, u = unit(j, c)
        remote(m_recv.at[u, :4], m_recv.at[u, :4], m_s, m_r.at[u, 3], partner).wait_recv()
        own_mid(j, c).wait()

    def partial(j, c):
        _, m_recv, p_send, p_recv, _, _, p_s, p_r, _, u = unit(j, c)
        for n, i in enumerate(X_DISTS + (0,)):
            col = (x + i) % NX
            a = full[j, pl.ds(pl.multiple_of(col * 2 * RANK, 2 * RANK), 2 * RANK)]
            p_send[u, col] = dot(a, m_recv[u].reshape(NZ * RANK, -1)).astype(BF16)
            if i:
                remote(p_send.at[u, col], p_recv.at[u, n], p_s, p_r.at[u], at_x(col)).start()

    def halves(j, c):
        _, _, p_send, p_recv, _, _, p_s, p_r, _, u = unit(j, c)
        remote(p_recv.at[u], p_recv.at[u], p_s, p_r.at[u], partner).wait_recv()
        total = p_send[u, x].astype(F32)
        for n in range(3):
            total += p_recv[u, n].astype(F32)
        half[j, :, cut(j, c)] = total.astype(BF16)

    def residual(c):
        for h in range(2):
            here = pl.ds(h * 4 * RANK, 4 * RANK)
            part = slice(h * RANK, (h + 1) * RANK)
            a = jnp.concatenate([outer_v[0, h], outer_v[1, h]], axis=1)
            b = jnp.concatenate([half[0, part, cut(0, c)], half[1, part, cut(1, c)]], axis=0)
            value = rhs_v[here, cut(0, c)].astype(F32) - dot(a, b)
            res[here, cut(0, c)] = value
            res_b[here, cut(0, c)] = value.astype(BF16)

    def finish(c):
        for h in range(2):
            here = pl.ds(h * 4 * RANK, 4 * RANK)
            value = res[here, cut(2, c)] + dot(outer_v[2, h], half[2, h * RANK : (h + 1) * RANK, cut(2, c)])
            out[0, here, cut(2, c)] = value.astype(BF16)

    send_second(0)
    outer_weights(0)
    outer_weights(1)
    outer_weights(2)
    loads[6].wait()
    for j in range(3):
        for l in range(4):
            leaf_t[j, l] = leaf_v[j, l].T
    loads[7].wait()
    loads[8].wait()
    for n, i in enumerate((1, 3, 2)):
        here = gath.at[:, ((y - i + NY) % NY) * 2 + core]
        remote(here, here, ag_s, ag_r.at[n], partner).wait_recv()
        remote(here, here, ag_s, ag_r.at[3], partner).start()
    remote(gath.at[:, :4], gath.at[:, :4], ag_s, ag_r.at[3], partner).wait_recv()
    for j in range(2):
        for c in range(EARLY):
            leaf_levels(j, c, lambda l: gath[j, 2 * l : 2 * l + 2, :, cut(j, c)].reshape(2 * RANK, -1))
            send_mid(j, c)
    send_second(1, 0, 1)
    full_weights(0)
    units = [(j, c) for j in range(2) for c in range(EARLY)]
    for n, (j, c) in enumerate(units):
        pass_mid(j, c)
        send_second(1, 1 + 6 * n // len(units), 1 + 6 * (n + 1) // len(units))
    send_second(2)
    for c in range(EARLY):
        wait_mid(0, c)
        partial(0, c)
    full_weights(1)
    for c in range(EARLY):
        wait_mid(1, c)
        partial(1, c)
    loads[9].wait()
    loads[10].wait()

    def start_late(c):
        leaf_levels(2, c, lambda l: res_b[l * 2 * RANK : (l + 1) * 2 * RANK, cut(2, c)])
        send_mid(2, c)

    for c in range(EARLY):
        halves(0, c)
        halves(1, c)
        residual(c)
        if c == 0:
            start_late(0)
            start_late(1)
    for c in range(LATE):
        pass_mid(2, c)
        if c + 2 < LATE:
            start_late(c + 2)
        if c == 0:
            full_weights(2)
        if c:
            wait_mid(2, c - 1)
            partial(2, c - 1)
    wait_mid(2, LATE - 1)
    partial(2, LATE - 1)
    for c in range(LATE):
        halves(2, c)
        finish(c)
    for there, sem in (
        (gath.at[:, :7], ag_s), (sec.at[:, :7], sec_s), (w_recv.at[:, :3], w_s),
        (m_recv0.at[:, :7], m_s0), (m_recv1.at[:, :7], m_s1), (p_recv0, p_s0), (p_recv1, p_s1),
    ):
        remote(there, there, sem, sem, partner).wait_send()


def on_device(*args):
    vmem = pltpu.VMEM
    dma = pltpu.SemaphoreType.DMA
    groups = ((2 * EARLY, EARLY), (LATE, LATE))
    return pl.pallas_call(
        kernel,
        out_shape=vmem((1, 1024, COLS), BF16),
        in_specs=[pl.BlockSpec(memory_space=pl.ANY)] * 8,
        out_specs=pl.BlockSpec(memory_space=pltpu.VMEM),
        scratch_shapes=[
            vmem((2, 8, RANK, COLS), BF16),
            vmem((3, 4, 2 * RANK, RANK), BF16),
            vmem((3, 4, RANK, 2 * RANK), BF16),
            vmem((3, 4, 4, RANK, RANK), BF16),
            vmem((3, 32, RANK, RANK), BF16),
            vmem((3, 2, NZ, RANK, RANK), BF16),
            vmem((3, 2, 4 * RANK, RANK), BF16),
            vmem((1024, COLS), BF16),
            vmem((3, NX, NZ, 2 * RANK, RANK), BF16),
            vmem((3, NX, NZ, 2 * RANK, RANK), BF16),
            vmem((3, NZ, NX, RANK, RANK), BF16),
            vmem((3, 8 * RANK, 8 * RANK), BF16),
            vmem((3, 2 * RANK, COLS), BF16),
            vmem((1024, COLS), F32),
            vmem((1024, COLS), BF16),
            *[ref for units, chunks in groups for ref in (
                vmem((units, 4, RANK, COLS // chunks), BF16),
                vmem((units, NZ, RANK, COLS // chunks), BF16),
                vmem((units, NX, 2 * RANK, COLS // chunks), BF16),
                vmem((units, 3, 2 * RANK, COLS // chunks), BF16),
            )],
            dma((12,)),
            dma((3,)),
            dma(()),
            dma((4,)),
            dma(()),
            dma((3,)),
            dma(()),
            dma((3,)),
            *[ref for units, _ in groups for ref in (
                dma(()), dma((units, 4)), dma(()), dma((units,)), dma((units,)),
            )],
        ],
        compiler_params=pltpu.CompilerParams(
            collective_id=0, has_side_effects=True, vmem_limit_bytes=60 << 20
        ),
    )(*args)


def solution(mesh):
    placed = (
        P(None, ("box", "row"), None),
        P("row", "box", None),
        P("row", None, "box", None, None),
        P("row", None, "box", None, None, None, None),
        P("row", None, "box", None, None, None),
        P("row", None, "box", None, None, None),
        P("row", None, "box", None, None, None, None),
        P("row", None, "box", None, None),
    )
    return jax.shard_map(on_device, mesh=mesh, in_specs=placed, out_specs=P("row", "box", None), check_vma=False)
```

```python
import functools

import jax
import jax.numpy as jnp
from jax import lax
from jax.experimental import pallas as pl
from jax.experimental.pallas import tpu as pltpu
from jax.sharding import PartitionSpec as P

F32 = jnp.float32
BF16 = jnp.bfloat16
MESH = pl.DeviceIdType.MESH
NX, NZ, NY = 4, 8, 4
X_DISTS = (2, 1, 3)
Z_DISTS = (1, 7, 2, 6, 3, 5, 4)
RANK, COLS = 128, 512
EARLY, LATE = 2, 4


def dot(a, b):
    return jnp.dot(a, b, preferred_element_type=F32)


def kernel(
    solved, rhs, leaf, first, second, third, fourth, outer, out,
    gath, leaf_v, leaf_t, first_v, third_v, fourth_v, outer_v, rhs_v,
    w_send, w_recv, sec, full, half, res, res_b,
    m_send0, m_recv0, p_send0, p_recv0, m_send1, m_recv1, p_send1, p_recv1,
    load_sem, own_sem, ag_s, ag_r, w_s, w_r, sec_s, sec_r,
    m_s0, m_r0, p_s0, p_r0, m_s1, m_r1, p_s1, p_r1,
):
    early = (m_send0, m_recv0, p_send0, p_recv0, m_s0, m_r0, p_s0, p_r0, EARLY, 0)
    late = (m_send1, m_recv1, p_send1, p_recv1, m_s1, m_r1, p_s1, p_r1, LATE, 2)

    def unit(j, c):
        *refs, chunks, base = late if j == 2 else early
        return (*refs, (j - base) * chunks + c)

    def cut(j, c):
        width = COLS // (LATE if j == 2 else EARLY)
        return slice(c * width, (c + 1) * width)

    row, box = lax.axis_index("row"), lax.axis_index("box")
    y, core = row // 2, row % 2
    z, x = box // NX, box % NX

    def at_z(plane):
        return (row, plane * NX + x)

    def at_x(col):
        return (row, z * NX + col)

    def at_y(chip):
        return (chip * 2 + core, box)

    partner = (y * 2 + 1 - core, box)
    other_z = z + 1 - 2 * (z % 2)

    def remote(src, dst, send, recv, device):
        return pltpu.make_async_remote_copy(
            src_ref=src, dst_ref=dst, send_sem=send, recv_sem=recv, device_id=device, device_id_type=MESH
        )

    barrier = pltpu.get_barrier_semaphore()
    peers = [partner] + [at_y((y + i) % NY) for i in range(1, NY)]
    peers += [at_x((x + i) % NX) for i in range(1, NX)] + [at_z((z + i) % NZ) for i in range(1, NZ)]
    for peer in peers:
        pl.semaphore_signal(barrier, inc=1, device_id=peer, device_id_type=MESH)

    loads = [
        (third.at[0, 0, 0], third_v.at[0]),
        (fourth.at[0, 0, 0], fourth_v.at[0]),
        (third.at[0, 1, 0], third_v.at[1]),
        (fourth.at[0, 1, 0], fourth_v.at[1]),
        (third.at[0, 2, 0], third_v.at[2]),
        (fourth.at[0, 2, 0], fourth_v.at[2]),
        (leaf.at[0], leaf_v),
        (first.at[0, :, 0], first_v),
        (solved, gath.at[:, row]),
        (outer.at[0], outer_v),
        (rhs.at[0], rhs_v),
        (second.at[0, :, 0, pl.ds(z * NX, NX)], sec.at[:, z]),
    ]
    loads = [pltpu.make_async_copy(src, dst, load_sem.at[i]) for i, (src, dst) in enumerate(loads)]
    for copy in loads:
        copy.start()
    pl.semaphore_wait(barrier, len(peers))

    for n, i in enumerate((1, 3, 2)):
        remote(solved, gath.at[:, row], ag_s, ag_r.at[n], at_y((y + i) % NY)).start()
    remote(solved, gath.at[:, row], ag_s, ag_r.at[3], partner).start()

    def send_second(j, begin=0, end=7):
        for i in Z_DISTS[begin:end]:
            plane = (z + i) % NZ
            remote(second.at[0, j, 0, pl.ds(plane * NX, NX)], sec.at[j, z], sec_s, sec_r.at[j], at_z(plane)).start()

    def wait_second(j):
        remote(sec.at[j, :7], sec.at[j, :7], sec_s, sec_r.at[j], partner).wait_recv()
        if j == 0:
            loads[11].wait()

    def outer_weights(j):
        loads[2 * j].wait()
        loads[2 * j + 1].wait()

        @pl.loop(0, NZ)
        def _(q):
            a = fourth_v[j, :, q].reshape(2 * RANK, RANK)
            b = jnp.concatenate([third_v[j, q * NX + k] for k in range(NX)], axis=1)
            o = dot(a, b).astype(BF16)
            for k in range(NX):
                w_send[j, k, q] = o[:, k * RANK : (k + 1) * RANK]

        for i in X_DISTS:
            col = (x + i) % NX
            remote(w_send.at[j, col], w_recv.at[j, x], w_s, w_r.at[j], at_x(col)).start()
        pltpu.make_async_copy(w_send.at[j, x], w_recv.at[j, x], own_sem.at[j]).start()

    def wait_weights(j):
        remote(w_recv.at[j, :3], w_recv.at[j, :3], w_s, w_r.at[j], partner).wait_recv()
        pltpu.make_async_copy(w_send.at[j, x], w_recv.at[j, x], own_sem.at[j]).wait()

    def full_weights(j):
        wait_second(j)
        wait_weights(j)

        @pl.loop(0, NX)
        def _(c):
            for q in range(NZ):
                full[j, pl.ds(c * 2 * RANK, 2 * RANK), q * RANK : (q + 1) * RANK] = dot(
                    w_recv[j, c, q], sec[j, q, c]
                ).astype(BF16)

    def leaf_levels(j, c, rows_of):
        m_send, *_, u = unit(j, c)
        coef = jnp.concatenate([dot(leaf_t[j, l], rows_of(l)).astype(BF16) for l in range(4)], axis=0)
        a = jnp.concatenate([first_v[j, :, k].reshape(4 * RANK, RANK) for k in range(4)], axis=1)
        m_send[u] = dot(a, coef).astype(BF16).reshape(4, RANK, -1)

    pair, odd = z // 2, z % 2
    near = [(z + 2 - odd) % NZ, (z + 5 - 2 * odd) % NZ, (z + 7 - odd) % NZ]
    side = 2 * odd - 1

    def send_mid(j, c):
        m_send, m_recv, _, _, m_s, m_r, _, _, u = unit(j, c)
        for t, (plane, n) in enumerate(zip(near, (1 - odd, 2, odd))):
            s = (pair + t + 1) % 4
            remote(m_send.at[u, s], m_recv.at[u, z], m_s, m_r.at[u, n], at_z(plane)).start()
        remote(m_send.at[u, pair], m_recv.at[u, z], m_s, m_r.at[u, 3], at_z(other_z)).start()
        m_recv[u, z] = m_send[u, pair]

    def pass_mid(j, c):
        _, m_recv, _, _, m_s, m_r, _, _, u = unit(j, c)
        for n, i in enumerate((1, 2, 3)):
            here = m_recv.at[u, (z + side * i + NZ) % NZ]
            remote(here, here, m_s, m_r.at[u, n], partner).wait_recv()
            remote(here, here, m_s, m_r.at[u, 3], at_z(other_z)).start()

    def wait_mid(j, c):
        _, m_recv, _, _, m_s, m_r, _, _, u = unit(j, c)
        remote(m_recv.at[u, :4], m_recv.at[u, :4], m_s, m_r.at[u, 3], partner).wait_recv()

    def partial(j, c):
        _, m_recv, p_send, p_recv, _, _, p_s, p_r, u = unit(j, c)
        for n, i in enumerate(X_DISTS + (0,)):
            col = (x + i) % NX
            a = full[j, pl.ds(pl.multiple_of(col * 2 * RANK, 2 * RANK), 2 * RANK)]
            p_send[u, col] = dot(a, m_recv[u].reshape(NZ * RANK, -1)).astype(BF16)
            if i:
                remote(p_send.at[u, col], p_recv.at[u, n], p_s, p_r.at[u], at_x(col)).start()

    def halves(j, c):
        _, _, p_send, p_recv, _, _, p_s, p_r, u = unit(j, c)
        remote(p_recv.at[u], p_recv.at[u], p_s, p_r.at[u], partner).wait_recv()
        total = p_send[u, x].astype(F32)
        for n in range(3):
            total += p_recv[u, n].astype(F32)
        half[j, :, cut(j, c)] = total.astype(BF16)

    def residual(c):
        for h in range(2):
            here = pl.ds(h * 4 * RANK, 4 * RANK)
            part = slice(h * RANK, (h + 1) * RANK)
            a = jnp.concatenate([outer_v[0, h], outer_v[1, h]], axis=1)
            b = jnp.concatenate([half[0, part, cut(0, c)], half[1, part, cut(1, c)]], axis=0)
            value = rhs_v[here, cut(0, c)].astype(F32) - dot(a, b)
            res[here, cut(0, c)] = value
            res_b[here, cut(0, c)] = value.astype(BF16)

    def finish(c):
        for h in range(2):
            here = pl.ds(h * 4 * RANK, 4 * RANK)
            value = res[here, cut(2, c)] + dot(outer_v[2, h], half[2, h * RANK : (h + 1) * RANK, cut(2, c)])
            out[0, here, cut(2, c)] = value.astype(BF16)

    send_second(0)
    outer_weights(0)
    outer_weights(1)
    outer_weights(2)
    loads[6].wait()
    for j in range(3):
        for l in range(4):
            leaf_t[j, l] = leaf_v[j, l].T
    loads[7].wait()
    loads[8].wait()
    for n, i in enumerate((1, 3, 2)):
        here = gath.at[:, ((y - i + NY) % NY) * 2 + core]
        remote(here, here, ag_s, ag_r.at[n], partner).wait_recv()
        remote(here, here, ag_s, ag_r.at[3], partner).start()
    remote(gath.at[:, :4], gath.at[:, :4], ag_s, ag_r.at[3], partner).wait_recv()
    for j in range(2):
        for c in range(EARLY):
            leaf_levels(j, c, lambda l: gath[j, 2 * l : 2 * l + 2, :, cut(j, c)].reshape(2 * RANK, -1))
            send_mid(j, c)
    send_second(1, 0, 1)
    full_weights(0)
    units = [(j, c) for j in range(2) for c in range(EARLY)]
    for n, (j, c) in enumerate(units):
        pass_mid(j, c)
        send_second(1, 1 + 6 * n // len(units), 1 + 6 * (n + 1) // len(units))
    send_second(2)
    for c in range(EARLY):
        wait_mid(0, c)
        partial(0, c)
    full_weights(1)
    for c in range(EARLY):
        wait_mid(1, c)
        partial(1, c)
    loads[9].wait()
    loads[10].wait()

    def start_late(c):
        leaf_levels(2, c, lambda l: res_b[l * 2 * RANK : (l + 1) * 2 * RANK, cut(2, c)])
        send_mid(2, c)

    for c in range(EARLY):
        halves(0, c)
        halves(1, c)
        residual(c)
        if c == 0:
            start_late(0)
            start_late(1)
    for c in range(LATE):
        pass_mid(2, c)
        if c + 2 < LATE:
            start_late(c + 2)
        if c == 0:
            full_weights(2)
        if c:
            wait_mid(2, c - 1)
            partial(2, c - 1)
    wait_mid(2, LATE - 1)
    partial(2, LATE - 1)
    for c in range(LATE):
        halves(2, c)
        finish(c)
    for there, sem in (
        (gath.at[:, :7], ag_s), (sec.at[:, :7], sec_s), (w_recv.at[:, :3], w_s),
        (m_recv0.at[:, :7], m_s0), (m_recv1.at[:, :7], m_s1), (p_recv0, p_s0), (p_recv1, p_s1),
    ):
        remote(there, there, sem, sem, partner).wait_send()


def on_device(*args):
    vmem = pltpu.VMEM
    dma = pltpu.SemaphoreType.DMA
    groups = ((2 * EARLY, EARLY), (LATE, LATE))
    return pl.pallas_call(
        kernel,
        out_shape=vmem((1, 1024, COLS), BF16),
        in_specs=[pl.BlockSpec(memory_space=pl.ANY)] * 8,
        out_specs=pl.BlockSpec(memory_space=pltpu.VMEM),
        scratch_shapes=[
            vmem((2, 8, RANK, COLS), BF16),
            vmem((3, 4, 2 * RANK, RANK), BF16),
            vmem((3, 4, RANK, 2 * RANK), BF16),
            vmem((3, 4, 4, RANK, RANK), BF16),
            vmem((3, 32, RANK, RANK), BF16),
            vmem((3, 2, NZ, RANK, RANK), BF16),
            vmem((3, 2, 4 * RANK, RANK), BF16),
            vmem((1024, COLS), BF16),
            vmem((3, NX, NZ, 2 * RANK, RANK), BF16),
            vmem((3, NX, NZ, 2 * RANK, RANK), BF16),
            vmem((3, NZ, NX, RANK, RANK), BF16),
            vmem((3, 8 * RANK, 8 * RANK), BF16),
            vmem((3, 2 * RANK, COLS), BF16),
            vmem((1024, COLS), F32),
            vmem((1024, COLS), BF16),
            *[ref for units, chunks in groups for ref in (
                vmem((units, 4, RANK, COLS // chunks), BF16),
                vmem((units, NZ, RANK, COLS // chunks), BF16),
                vmem((units, NX, 2 * RANK, COLS // chunks), BF16),
                vmem((units, 3, 2 * RANK, COLS // chunks), BF16),
            )],
            dma((12,)),
            dma((3,)),
            dma(()),
            dma((4,)),
            dma(()),
            dma((3,)),
            dma(()),
            dma((3,)),
            *[ref for units, _ in groups for ref in (
                dma(()), dma((units, 4)), dma(()), dma((units,)),
            )],
        ],
        compiler_params=pltpu.CompilerParams(
            collective_id=0, has_side_effects=True, vmem_limit_bytes=60 << 20
        ),
    )(*args)


def solution(mesh):
    placed = (
        P(None, ("box", "row"), None),
        P("row", "box", None),
        P("row", None, "box", None, None),
        P("row", None, "box", None, None, None, None),
        P("row", None, "box", None, None, None),
        P("row", None, "box", None, None, None),
        P("row", None, "box", None, None, None, None),
        P("row", None, "box", None, None),
    )
    return jax.shard_map(on_device, mesh=mesh, in_specs=placed, out_specs=P("row", "box", None), check_vma=False)
```
